256 devices in a mesh: dp: 4 (over y), vocab: 64 (over x, z, core).
Axes of the slice: x: 4, y: 4, z: 8, core: 2. Of those that a mesh axis runs over, the one named last changes fastest.
Arguments:
- hidden: bfloat16 [2048, 4096], P(('dp', 'vocab')), may hold values from -250 to 250
- targets: int32 [2048], P(('dp', 'vocab')), may hold values from 0 to 501759, as said below
- loss_weight: bfloat16 [2048], P(('dp', 'vocab')), may hold values from 0.5 to 2
- head_weight: bfloat16 [4096, 10240], P(None, 'vocab'), may hold values from -0.09375 to 0.09375
- cluster_weight: bfloat16 [4096, 64], P(None, 'vocab'), may hold values from -0.09375 to 0.09375
- tail_proj: bfloat16 [64, 4096, 1024], P('vocab', None, 'dp'), may hold values from -0.09375 to 0.09375
- tail_out: bfloat16 [64, 1024, 7680], P('vocab', 'dp'), may hold values from -0.1875 to 0.1875
Outputs:
- hidden_grad: bfloat16 [2048, 4096], P(('dp', 'vocab'))
- head_grad: bfloat16 [4096, 10240], P('dp', 'vocab')
- cluster_grad: bfloat16 [4096, 64], P('dp', 'vocab')
- proj_grad: bfloat16 [64, 4096, 1024], P('vocab', None, 'dp')
- out_grad: bfloat16 [64, 1024, 7680], P('vocab', 'dp')
The draws below stay inside these ranges and needn't reach their ends.
Inputs may be any that keep to these rules, and one draw needn't show every extreme that they name: In each block of 512 consecutive tokens exactly 256 targets are at or above 10240; at most 16 of them fall in one cluster, and some cluster holds exactly 16 of them in every block.
All inputs are finite; a program needn't handle non-finite values.
Results may differ from the reference program's by a relative error of at most 0.012.
The reference program's roundings to bfloat16 on the way count: a program that leaves them out, or rounds other values in their place, can miss the bound.
Values may be sent and summed in bfloat16 or wider, within the bound.
No kernel may reach another device: no remote copies, remote signals or barrier semaphores. Data moves between devices by JAX's collectives and lax.ppermute only.
A program may use at most 128 MiB of HBM per device.

```python
import math
import jax
import jax.numpy as jnp
from jax import lax

MODEL_DIMENSION = 4096
HEAD = 10240
PROJ = 1024
CV = 7680
CLUSTER_TOKEN_CAP = 16
CLUSTERS = 64
TOK_ROW = 512
TOKENS = 2048
N_DP = 4


def draw_hidden(key, part):
    base = jax.random.normal(jax.random.fold_in(key, 5), (TOKENS, MODEL_DIMENSION), jnp.float32)
    base = jnp.clip(base, -6.0, 6.0)
    return base.astype(jnp.bfloat16)


def draw_targets(key, part):
    cluster_groups = TOKENS // TOK_ROW
    slots = CLUSTERS * CLUSTER_TOKEN_CAP
    owner = jnp.arange(slots, dtype=jnp.int32) // CLUSTER_TOKEN_CAP

    def one_block(index):
        block_key = jax.random.fold_in(jax.random.fold_in(key, 17), index)
        keys = jax.random.split(block_key, 6)
        heat = jax.random.randint(keys[0], (CLUSTERS,), 0, 4)
        hottest = jax.random.randint(keys[1], (), 0, CLUSTERS)
        noise = jax.random.randint(keys[2], (slots,), 0, 4096)
        score = heat[owner] * 1536 + noise
        score = jnp.where(owner == hottest, 32768, score)
        score = score * slots + jnp.arange(slots, dtype=jnp.int32)
        unused, chosen = lax.top_k(score, TOK_ROW // 2)
        picked = owner[chosen]
        order = jax.random.permutation(keys[3], TOK_ROW)
        cluster = jnp.full((TOK_ROW,), -1, jnp.int32).at[order[:TOK_ROW // 2]].set(picked)
        head_word = jax.random.randint(keys[4], (TOK_ROW,), 0, HEAD)
        tail_word = jax.random.randint(keys[5], (TOK_ROW,), 0, CV)
        return jnp.where(cluster < 0, head_word, HEAD + cluster * CV + tail_word)
    return jax.vmap(one_block)(jnp.arange(cluster_groups)).reshape(TOKENS).astype(jnp.int32)


def block_scale(stream_key, extent, pieces, low, high):
    def one(position, shards_of):
        heights = jax.random.uniform(jax.random.fold_in(jax.random.fold_in(stream_key, 6), position), (shards_of,), jnp.float32, low / len(pieces), high / len(pieces))
        return jnp.repeat(jnp.exp(heights), extent[position] // shards_of).reshape((-1,) + (1,) * (len(extent) - position - 1))

    level = one(*pieces[0])
    for cut in pieces[1:]:
        level = level * one(*cut)
    return level


def centred(stream_key, shape, scale, limit, shards=(), held_as=jnp.bfloat16):
    level = block_scale(stream_key, shape, shards, -0.22, 0.18) if shards else 1.0
    result = jax.random.normal(stream_key, shape, jnp.float32) * scale * level
    return jnp.minimum(jnp.maximum(result, -limit), limit).astype(held_as)


def setup_inputs(seed: int = 0) -> dict:
    splits = jax.random.split(jax.random.key(seed), 8)
    hidden = draw_hidden(jax.random.fold_in(splits[7], 71), 0)
    targets = draw_targets(jax.random.fold_in(splits[7], 71), 0)
    loss_weight = jnp.clip(jnp.exp(math.log(2.0) - 1.3862944 * jax.random.uniform(splits[2], (TOKENS,), jnp.float32) ** block_scale(splits[2], (TOKENS,), ((0, 256),), -0.2, 0.2)), 0.5, 2.0).astype(jnp.bfloat16)
    head_weight = centred(splits[3], (MODEL_DIMENSION, HEAD), MODEL_DIMENSION ** -0.5, 0.09375, ((1, 64),))
    cluster_weight = centred(splits[4], (MODEL_DIMENSION, CLUSTERS), MODEL_DIMENSION ** -0.5, 0.09375, ((1, 64),))
    tail_proj = centred(splits[5], (CLUSTERS, MODEL_DIMENSION, PROJ), MODEL_DIMENSION ** -0.5, 0.09375, ((0, 64), (2, 4)))
    tail_out = centred(splits[6], (CLUSTERS, PROJ, CV), PROJ ** -0.5, 0.1875, ((0, 64), (1, 4)))
    return dict(hidden=hidden, targets=targets, loss_weight=loss_weight, head_weight=head_weight, cluster_weight=cluster_weight, tail_proj=tail_proj, tail_out=tail_out)


def pick_rows(hidden_block_list, target_blocks, weight_blocks, cluster):
    offset = target_blocks - HEAD
    member = (offset >= 0) & (offset // CV == cluster)
    rank = jnp.cumsum(member.astype(jnp.int32), axis=1) - 1
    slots = jnp.arange(CLUSTER_TOKEN_CAP, dtype=jnp.int32)
    select = member[:, None, :] & (rank[:, None, :] == slots[None, :, None])
    cluster_selector = select.astype(jnp.float32)
    token_row_list = jnp.einsum("ahw,awo->aho", cluster_selector, hidden_block_list.astype(jnp.float32), precision=lax.Precision.HIGHEST)
    words = jnp.sum(jnp.where(select, (offset % CV)[:, None, :], 0), axis=2).astype(jnp.int32)
    gains = jnp.sum(jnp.where(select, weight_blocks.astype(jnp.float32)[:, None, :], 0.0), axis=2)
    return token_row_list.astype(jnp.bfloat16), words, gains, cluster_selector


def reference(hidden, targets, loss_weight, head_weight, cluster_weight, tail_proj, tail_out):
    gain = loss_weight.astype(jnp.float32)
    every_weight = jnp.concatenate([head_weight, cluster_weight], axis=1)
    logits = jnp.dot(hidden, every_weight, preferred_element_type=jnp.float32)
    offset = targets - HEAD
    target_column = jnp.where(offset >= 0, HEAD + offset // CV, targets).astype(jnp.int32)
    top = jnp.max(logits, axis=1, keepdims=True)
    expo = jnp.exp(logits - top)
    prob = expo / jnp.sum(expo, axis=1, keepdims=True)
    columns = jnp.arange(logits.shape[1], dtype=jnp.int32)
    onehot = (columns[None, :] == target_column[:, None]).astype(jnp.float32)
    delta = (gain[:, None] * (prob - onehot)).astype(jnp.bfloat16)
    head_part = lax.dot_general(delta, every_weight, (((1,), (1,)), ((), ())), preferred_element_type=jnp.float32)
    weight_grad = lax.dot_general(hidden, delta, (((0,), (0,)), ((), ())), preferred_element_type=jnp.float32).astype(jnp.bfloat16)
    cluster_groups = N_DP
    span = TOKENS // N_DP
    hidden_block_list = hidden.reshape(cluster_groups, span, MODEL_DIMENSION)
    target_blocks = targets.reshape(cluster_groups, span)
    weight_blocks = loss_weight.reshape(cluster_groups, span)
    word_columns = jnp.arange(CV, dtype=jnp.int32)

    def one_cluster(carry, inputs):
        cluster, proj, out = inputs
        token_row_list, words, gains, cluster_selector = pick_rows(hidden_block_list, target_blocks, weight_blocks, cluster)
        token_row_list = token_row_list.reshape(cluster_groups * CLUSTER_TOKEN_CAP, MODEL_DIMENSION)
        words = words.reshape(cluster_groups * CLUSTER_TOKEN_CAP)
        gains = gains.reshape(cluster_groups * CLUSTER_TOKEN_CAP)
        reduced = jnp.dot(token_row_list, proj, preferred_element_type=jnp.float32).astype(jnp.bfloat16)
        word_logits = jnp.dot(reduced, out, preferred_element_type=jnp.float32)
        word_top = jnp.max(word_logits, axis=1, keepdims=True)
        word_exp = jnp.exp(word_logits - word_top)
        word_prob = word_exp / jnp.sum(word_exp, axis=1, keepdims=True)
        word_hot = (word_columns[None, :] == words[:, None]).astype(jnp.float32)
        word_delta = (gains[:, None] * (word_prob - word_hot)).astype(jnp.bfloat16)
        reduced_grad = lax.dot_general(word_delta, out, (((1,), (1,)), ((), ())), preferred_element_type=jnp.float32).astype(jnp.bfloat16)
        out_grad = lax.dot_general(reduced, word_delta, (((0,), (0,)), ((), ())), preferred_element_type=jnp.float32).astype(jnp.bfloat16)
        proj_grad = lax.dot_general(token_row_list, reduced_grad, (((0,), (0,)), ((), ())), preferred_element_type=jnp.float32).astype(jnp.bfloat16)
        tail_portion = lax.dot_general(reduced_grad, proj, (((1,), (1,)), ((), ())), preferred_element_type=jnp.float32)
        backward_result = jnp.einsum("vpg,vpl->vgl", cluster_selector, tail_portion.reshape(cluster_groups, CLUSTER_TOKEN_CAP, MODEL_DIMENSION), precision=lax.Precision.HIGHEST)
        return carry + backward_result, (proj_grad, out_grad)

    start = jnp.zeros((cluster_groups, span, MODEL_DIMENSION), jnp.float32)
    cluster_ids = jnp.arange(CLUSTERS, dtype=jnp.int32)
    tail_back, grads = lax.scan(one_cluster, start, (cluster_ids, tail_proj, tail_out))
    proj_grad, out_grad = grads
    hidden_grad = (head_part + tail_back.reshape(TOKENS, MODEL_DIMENSION)).astype(jnp.bfloat16)
    return hidden_grad, weight_grad[:, :HEAD], weight_grad[:, HEAD:], proj_grad, out_grad
```

```python
import jax
import jax.numpy as jnp
from jax import lax
from jax.sharding import Mesh
from jax.sharding import PartitionSpec as P

HEAD = 10240
CV = 7680
CAP = 16
OWN = 8
NX, NZ, NDP = 4, 8, 4
CA = 1792
META = 128


F32, BF16 = jnp.float32, jnp.bfloat16


def shift(value, axis, step):
    n = lax.axis_size(axis)
    return lax.ppermute(value, axis, [(j, (j + step) % n) for j in range(n)])


def dot(a, b, ca=1, cb=0):
    return lax.dot_general(a, b, (((ca,), (cb,)), ((), ())), preferred_element_type=F32)


def gathered(hidden, targets, loss_weight):
    digits = jnp.stack(
        [
            (targets >> 16).astype(BF16),
            ((targets >> 8) & 255).astype(BF16),
            (targets & 255).astype(BF16),
            loss_weight,
        ],
        axis=1,
    )
    meta = jnp.pad(digits, ((0, 0), (0, META - 4)))
    pay_a = hidden[:, :CA]
    pay_b = jnp.concatenate([hidden[:, CA:], meta], axis=1)
    b1 = jnp.concatenate([pay_b] + [shift(pay_b, "z", s) for s in range(1, NZ)], axis=0)
    a1 = jnp.concatenate([pay_a] + [shift(pay_a, "x", k) for k in range(1, NX)], axis=0)
    a2 = [a1] + [shift(a1, "z", s) for s in range(1, NZ)]
    own_a = jnp.concatenate([p.reshape(NX, 1, OWN, CA) for p in a2], axis=1)
    own_a = own_a.reshape(NX * NZ * OWN, CA)
    own_b = jnp.concatenate([b1] + [shift(b1, "x", k) for k in range(1, NX)], axis=0)
    return [own_a, shift(own_a, "core", 1)], [own_b, shift(own_b, "core", 1)]


def merge_soft(parts):
    top = parts[0][0]
    for p in parts[1:]:
        top = jnp.maximum(top, p[0])
    total = sum(p[1] * jnp.exp(p[0] - top) for p in parts)
    return jnp.stack([top, total])


def joined_stats(top, total):
    stats = jnp.stack([top, total]).reshape(2, 2, NX, NZ * OWN)
    stats = merge_soft([stats, jnp.roll(shift(stats, "core", 1), 1, axis=1)])
    stats = merge_soft(
        [stats] + [jnp.roll(shift(stats, "x", k), k, axis=2) for k in range(1, NX)]
    )
    stats = merge_soft(
        [stats] + [jnp.roll(shift(stats, "z", s), s * OWN, axis=3) for s in range(1, NZ)]
    )
    stats = stats.reshape(2, 2 * NX * NZ * OWN)
    return stats[0], stats[1]


def scattered(own_a, far_a, own_b, far_b):
    sum_a = own_a + shift(far_a, "core", 1).astype(F32)
    sum_b = own_b + shift(far_b, "core", 1).astype(F32)
    sum_a = sum_a.reshape(NX, NZ, OWN, CA)
    acc_a = sum_a[:, 0]
    for s in range(1, NZ):
        acc_a = acc_a + shift(sum_a[:, s].astype(BF16), "z", -s).astype(F32)
    rows = NZ * OWN
    acc_b = sum_b[:rows]
    for k in range(1, NX):
        acc_b = acc_b + shift(sum_b[k * rows : (k + 1) * rows].astype(BF16), "x", -k).astype(F32)
    out_a = acc_a[0]
    for k in range(1, NX):
        out_a = out_a + shift(acc_a[k].astype(BF16), "x", -k).astype(F32)
    out_b = acc_b[:OWN]
    for s in range(1, NZ):
        out_b = out_b + shift(acc_b[s * OWN : (s + 1) * OWN].astype(BF16), "z", -s).astype(F32)
    return jnp.concatenate([out_a, out_b], axis=1).astype(BF16)


def target_of(meta):
    meta = meta.astype(F32)
    return (meta[:, 0] * 65536.0 + meta[:, 1] * 256.0 + meta[:, 2]).astype(jnp.int32)


def shards(hidden, targets, loss_weight, head_weight, cluster_weight, tail_proj, tail_out):
    vocab_index = lax.axis_index(("x", "z", "core"))
    dp_index = lax.axis_index("dp")
    width = head_weight.shape[1]
    every_weight = jnp.concatenate([head_weight, cluster_weight], axis=1)
    weight_a = every_weight[:CA]
    weight_b = every_weight[CA:]
    weight_b_meta = jnp.pad(weight_b, ((0, META), (0, 0)))
    cb = weight_b.shape[0]
    half_a, half_b = gathered(hidden, targets, loss_weight)
    meta = jnp.concatenate([half_b[0][:, cb : cb + 4], half_b[1][:, cb : cb + 4]], axis=0)
    target = target_of(meta)
    gain = meta[:, 3].astype(F32)
    offset = target - HEAD
    span = target.shape[0]
    side = span // 2

    member = (offset >= 0) & (offset // CV == vocab_index)
    rank = jnp.cumsum(member.astype(jnp.int32)) - 1
    slots = jnp.arange(CAP, dtype=jnp.int32)
    select = (member[None, :] & (rank[None, :] == slots[:, None])).astype(BF16)
    sel = [select[:, :side], select[:, side:]]
    picked_a = (dot(sel[0], half_a[0]) + dot(sel[1], half_a[1])).astype(BF16)
    picked_b = (dot(sel[0], half_b[0]) + dot(sel[1], half_b[1])).astype(BF16)
    words = (target_of(picked_b[:, cb:]) - HEAD) % CV
    gain_tail = picked_b[:, cb + 3].astype(F32)
    rows = jnp.concatenate([picked_a, picked_b[:, :cb]], axis=1)
    tail_rows = jnp.concatenate([rows] + [shift(rows, "dp", k) for k in range(1, NDP)], axis=0)

    proj = tail_proj[0]
    out = tail_out[0]
    reduced = dot(tail_rows, proj).astype(BF16)
    partial = dot(reduced, out)
    share = partial[:CAP]
    for k in range(1, NDP):
        share = share + shift(partial[k * CAP : (k + 1) * CAP], "dp", -k)
    share_top = jnp.max(share, axis=1, keepdims=True)
    share_exp = jnp.exp(share - share_top)
    share_total = jnp.sum(share_exp, axis=1, keepdims=True)
    word_hot = (jnp.arange(CV, dtype=jnp.int32)[None, :] == words[:, None]).astype(F32)
    share_delta = (gain_tail[:, None] * (share_exp / share_total - word_hot)).astype(BF16)
    word_delta = jnp.concatenate(
        [share_delta] + [shift(share_delta, "dp", k) for k in range(1, NDP)], axis=0
    )
    reduced_grad = dot(word_delta, out, 1, 1).astype(BF16)
    tail_partial = dot(reduced_grad, proj, 1, 1)
    tail_sum = tail_partial[:CAP]
    for k in range(1, NDP):
        tail_sum = tail_sum + shift(
            tail_partial[k * CAP : (k + 1) * CAP].astype(BF16), "dp", -k
        ).astype(F32)
    tail_sum = tail_sum.astype(BF16)

    logits = jnp.concatenate(
        [dot(half_a[c], weight_a) + dot(half_b[c], weight_b_meta) for c in range(2)], axis=0
    )
    lane = jnp.arange(width + 1, dtype=jnp.int32)
    columns = jnp.where(lane < width, vocab_index * width + lane, HEAD + vocab_index)
    target_column = jnp.where(offset >= 0, HEAD + offset // CV, target)
    top = jnp.max(logits, axis=1)
    total = jnp.sum(jnp.exp(logits - top[:, None]), axis=1)
    top, total = joined_stats(top, total)
    hot = (columns[None, :] == target_column[:, None]).astype(F32)
    delta = (
        gain[:, None] * (jnp.exp(logits - top[:, None]) / total[:, None] - hot)
    ).astype(BF16)
    near, far = delta[:side], delta[side:]

    def token_partial(d, s, w, t):
        return dot(d, w, 1, 1) + dot(s, t, 0, 0)

    far_a = token_partial(far, sel[1], weight_a, tail_sum[:, :CA]).astype(BF16)
    far_b = token_partial(far, sel[1], weight_b, tail_sum[:, CA:]).astype(BF16)
    own_a = token_partial(near, sel[0], weight_a, tail_sum[:, :CA])
    own_b = token_partial(near, sel[0], weight_b, tail_sum[:, CA:])
    hidden_grad = scattered(own_a, far_a, own_b, far_b)

    late_delta, _ = lax.optimization_barrier((delta, tail_sum))
    near, far = late_delta[:side], late_delta[side:]
    grad_t = jnp.concatenate(
        [
            dot(near, half_a[0], 0, 0) + dot(far, half_a[1], 0, 0),
            (dot(near, half_b[0], 0, 0) + dot(far, half_b[1], 0, 0))[:, :cb],
        ],
        axis=1,
    ).astype(BF16)
    block = grad_t.shape[1] // NDP
    head_sum = 0.0
    for k in range(NDP):
        piece = lax.dynamic_slice_in_dim(grad_t, lax.rem(dp_index - k + NDP, NDP) * block, block, 1)
        head_sum = head_sum + (shift(piece, "dp", -k) if k else piece).astype(F32)
    head_sum = head_sum.astype(BF16)
    out_grad = dot(reduced, word_delta, 0, 0).astype(BF16)
    proj_grad = dot(tail_rows, reduced_grad, 0, 0).astype(BF16)
    return (
        hidden_grad,
        head_sum[:width].T,
        head_sum[width:].T,
        proj_grad[None],
        out_grad[None],
    )


def solution(mesh):
    fine = Mesh(mesh.devices.reshape(NDP, NX, NZ, 2), ("dp", "x", "z", "core"))
    vocab = ("x", "z", "core")
    return jax.shard_map(
        shards,
        mesh=fine,
        in_specs=(
            P(("dp", *vocab), None),
            P(("dp", *vocab)),
            P(("dp", *vocab)),
            P(None, vocab),
            P(None, vocab),
            P(vocab, None, "dp"),
            P(vocab, "dp", None),
        ),
        out_specs=(
            P(("dp", *vocab), None),
            P("dp", vocab),
            P("dp", vocab),
            P(vocab, None, "dp"),
            P(vocab, "dp", None),
        ),
        check_vma=False,
    )
```

```python
import jax
import jax.numpy as jnp
from jax import lax
from jax.sharding import Mesh
from jax.sharding import PartitionSpec as P


HEAD = 10240
CV = 7680
CAP = 16
OWN = 8
NX, NZ, NDP = 4, 8, 4
CA = 2048
META = 128


F32, BF16 = jnp.float32, jnp.bfloat16


def shift(value, axis, step):
    n = lax.axis_size(axis)
    return lax.ppermute(value, axis, [(j, (j + step) % n) for j in range(n)])


def dot(a, b, ca=1, cb=0):
    return lax.dot_general(a, b, (((ca,), (cb,)), ((), ())), preferred_element_type=F32)


def swapped(parts, axis):
    return lax.all_to_all(parts, axis, split_axis=0, concat_axis=0, tiled=True)


def from_everyone(value, axis):
    return swapped(jnp.broadcast_to(value, (lax.axis_size(axis), *value.shape)), axis)


def gathered(hidden, targets, loss_weight):
    digits = jnp.stack(
        [
            (targets >> 16).astype(BF16),
            ((targets >> 8) & 255).astype(BF16),
            (targets & 255).astype(BF16),
            loss_weight,
        ],
        axis=1,
    )
    meta = jnp.pad(digits, ((0, 0), (0, META - 4)))
    pay_a = hidden[:, :CA]
    pay_b = jnp.concatenate([hidden[:, CA:], meta], axis=1)
    half = NX * NZ * OWN
    a1 = jnp.concatenate([pay_a] + [shift(pay_a, "x", -k) for k in range(1, NX)], axis=0)
    b1 = from_everyone(pay_b, "z").reshape(NZ * OWN, -1)
    a1, b1 = lax.optimization_barrier((a1, b1))
    a2 = from_everyone(a1, "z").reshape(NZ, NX, OWN, CA)
    own_a = jnp.swapaxes(a2, 0, 1).reshape(half, CA)
    own_b = jnp.concatenate([b1] + [shift(b1, "x", -k) for k in range(1, NX)], axis=0)
    other_a = shift(own_a, "core", 1)
    other_b = shift(own_b, "core", 1)
    return [own_a, other_a], [own_b, other_b]


def joined_stats(top, total):
    first = lax.axis_index("core") == 0
    place = lax.axis_index("x")

    def turned(stats, start):
        stats = jnp.where(first, stats, stats[:, ::-1])
        return lax.dynamic_slice_in_dim(jnp.concatenate([stats] * 2, axis=2), start, NX, 2)

    shape = (2, 2, NX, NZ * OWN)
    stats = turned(jnp.stack([top, total]).reshape(shape), lax.rem(NX - place, NX))
    every = from_everyone(stats.reshape(2, -1), ("x", "z", "core"))
    top = jnp.max(every[:, 0], axis=0)
    total = jnp.sum(every[:, 1] * jnp.exp(every[:, 0] - top), axis=0)
    stats = turned(jnp.stack([top, total]).reshape(shape), place).reshape(2, -1)
    return stats[0], stats[1]


def summed_z(parts):
    parts = swapped(parts.astype(BF16), "z")
    return jnp.sum(parts.astype(F32), axis=0)


def summed_x(parts):
    parts_16 = parts.astype(BF16)
    total = parts[0]
    for k in range(1, NX):
        total = total + shift(parts_16[k], "x", k).astype(F32)
    return total


def scattered(sum_a, sum_b):
    a = jnp.swapaxes(sum_a.reshape(NX, NZ, OWN, CA), 0, 1).reshape(NZ, NX * OWN, CA)
    b = sum_b.reshape(NX, NZ * OWN, -1)
    a = summed_z(a).reshape(NX, OWN, CA)
    b = summed_x(b).reshape(NZ, OWN, -1)
    b = summed_z(b)
    a = summed_x(a)
    return jnp.concatenate([a, b], axis=1).astype(BF16)


def target_of(meta):
    meta = meta.astype(F32)
    return (meta[:, 0] * 65536.0 + meta[:, 1] * 256.0 + meta[:, 2]).astype(jnp.int32)


def step(hidden, targets, loss_weight, head_weight, cluster_weight, tail_proj, tail_out):
    vocab_index = lax.axis_index(("x", "z", "core"))
    dp_index = lax.axis_index("dp")
    width = head_weight.shape[1]
    every_weight = jnp.concatenate([head_weight, cluster_weight], axis=1)
    weight_a = every_weight[:CA]
    weight_b = every_weight[CA:]
    weight_b_meta = jnp.pad(weight_b, ((0, META), (0, 0)))
    cb = weight_b.shape[0]
    half_a, half_b = gathered(hidden, targets, loss_weight)
    meta = jnp.concatenate([half_b[0][:, cb : cb + 4], half_b[1][:, cb : cb + 4]], axis=0)
    target = target_of(meta)
    gain = meta[:, 3].astype(F32)
    offset = target - HEAD
    span = target.shape[0]
    side = span // 2

    member = (offset >= 0) & (offset // CV == vocab_index)
    at = jnp.arange(span, dtype=jnp.int32)
    ahead = (at[:, None] < at[None, :]).astype(jnp.int32)
    ahead = jnp.where(at[:, None] == at[None, :], span, ahead)
    code = jnp.sum(jnp.where(member[:, None], ahead, 0), axis=0)
    slots = jnp.arange(CAP, dtype=jnp.int32)
    select = (code[None, :] == slots[:, None] + span).astype(BF16)
    sel = [select[:, :side], select[:, side:]]
    picked_a = (dot(sel[0], half_a[0]) + dot(sel[1], half_a[1])).astype(BF16)
    picked_b = (dot(sel[0], half_b[0]) + dot(sel[1], half_b[1])).astype(BF16)
    words = (target_of(picked_b[:, cb:]) - HEAD) % CV
    gain_tail = picked_b[:, cb + 3].astype(F32)
    rows = jnp.concatenate([picked_a, picked_b[:, :cb]], axis=1)
    tail_rows = jnp.concatenate([rows] + [shift(rows, "dp", k) for k in range(1, NDP)], axis=0)

    proj = tail_proj[0]
    out = tail_out[0]
    reduced = dot(tail_rows, proj).astype(BF16)
    partial = dot(reduced, out)
    share = partial[:CAP]
    for k in range(1, NDP):
        share = share + shift(partial[k * CAP : (k + 1) * CAP], "dp", -k)
    share_top = jnp.max(share, axis=1, keepdims=True)
    share_exp = jnp.exp(share - share_top)
    share_total = jnp.sum(share_exp, axis=1, keepdims=True)
    word_hot = (jnp.arange(CV, dtype=jnp.int32)[None, :] == words[:, None]).astype(F32)
    share_delta = (gain_tail[:, None] * (share_exp / share_total - word_hot)).astype(BF16)
    word_delta = jnp.concatenate(
        [share_delta] + [shift(share_delta, "dp", k) for k in range(1, NDP)], axis=0
    )
    reduced_grad = dot(word_delta, out, 1, 1).astype(BF16)
    tail_partial = dot(reduced_grad, proj, 1, 1)
    tail_sum = tail_partial[:CAP]
    for k in range(1, NDP):
        tail_sum = tail_sum + shift(
            tail_partial[k * CAP : (k + 1) * CAP].astype(BF16), "dp", -k
        ).astype(F32)
    tail_sum = tail_sum.astype(BF16)

    (half_a, half_b), _ = lax.optimization_barrier(((half_a, half_b), rows))
    logits = jnp.concatenate(
        [dot(half_a[c], weight_a) + dot(half_b[c], weight_b_meta) for c in range(2)], axis=0
    )
    lane = jnp.arange(width + 1, dtype=jnp.int32)
    columns = jnp.where(lane < width, vocab_index * width + lane, HEAD + vocab_index)
    target_column = jnp.where(offset >= 0, HEAD + offset // CV, target)
    top = jnp.max(logits, axis=1)
    total = jnp.sum(jnp.exp(logits - top[:, None]), axis=1)
    top, total = joined_stats(top, total)
    hot = (columns[None, :] == target_column[:, None]).astype(F32)
    delta = (
        gain[:, None] * (jnp.exp(logits - top[:, None]) / total[:, None] - hot)
    ).astype(BF16)
    near, far = delta[:side], delta[side:]

    def token_partial(d, s, w, t):
        return dot(d, w, 1, 1) + dot(s, t, 0, 0)

    far_a = token_partial(far, sel[1], weight_a, tail_sum[:, :CA]).astype(BF16)
    far_b = token_partial(far, sel[1], weight_b, tail_sum[:, CA:]).astype(BF16)
    got_a = shift(far_a, "core", 1)
    got_b = shift(far_b, "core", 1)
    own_a = token_partial(near, sel[0], weight_a, tail_sum[:, :CA])
    own_b = token_partial(near, sel[0], weight_b, tail_sum[:, CA:])
    hidden_grad = scattered(own_a + got_a.astype(F32), own_b + got_b.astype(F32))

    grad_t = jnp.concatenate(
        [
            dot(near, half_a[0], 0, 0) + dot(far, half_a[1], 0, 0),
            (dot(near, half_b[0], 0, 0) + dot(far, half_b[1], 0, 0))[:, :cb],
        ],
        axis=1,
    ).astype(BF16)
    block = grad_t.shape[1] // NDP
    head_sum = 0.0
    for k in range(NDP):
        piece = lax.dynamic_slice_in_dim(grad_t, lax.rem(dp_index + k, NDP) * block, block, 1)
        head_sum = head_sum + (shift(piece, "dp", k) if k else piece).astype(F32)
    head_sum = head_sum.astype(BF16)
    out_grad = dot(reduced, word_delta, 0, 0).astype(BF16)
    proj_grad = dot(tail_rows, reduced_grad, 0, 0).astype(BF16)
    return (
        hidden_grad,
        head_sum[:width].T,
        head_sum[width:].T,
        proj_grad[None],
        out_grad[None],
    )


def solution(mesh):
    fine = Mesh(mesh.devices.reshape(NDP, NX, NZ, 2), ("dp", "x", "z", "core"))
    vocab = ("x", "z", "core")
    return jax.shard_map(
        step,
        mesh=fine,
        in_specs=(
            P(("dp", *vocab), None),
            P(("dp", *vocab)),
            P(("dp", *vocab)),
            P(None, vocab),
            P(None, vocab),
            P(vocab, None, "dp"),
            P(vocab, "dp", None),
        ),
        out_specs=(
            P(("dp", *vocab), None),
            P("dp", vocab),
            P("dp", vocab),
            P(vocab, None, "dp"),
            P(vocab, "dp", None),
        ),
        check_vma=False,
    )
```

```python
import jax
import jax.numpy as jnp
from jax import lax
from jax.sharding import Mesh
from jax.sharding import PartitionSpec as P


HEAD = 10240
CV = 7680
CAP = 16
OWN = 8
NX, NZ, NDP = 4, 8, 4
META = 128


F32, BF16 = jnp.float32, jnp.bfloat16


def shift(value, axis, step):
    n = lax.axis_size(axis)
    return lax.ppermute(value, axis, [(j, (j + step) % n) for j in range(n)])


def dot(a, b, ca=1, cb=0):
    return lax.dot_general(a, b, (((ca,), (cb,)), ((), ())), preferred_element_type=F32)


def swapped(parts, axis):
    return lax.all_to_all(parts, axis, split_axis=0, concat_axis=0, tiled=True)


def from_everyone(value, axis):
    return swapped(jnp.broadcast_to(value, (lax.axis_size(axis), *value.shape)), axis)


def gathered(hidden, targets, loss_weight):
    digits = jnp.stack(
        [
            (targets >> 16).astype(BF16),
            ((targets >> 8) & 255).astype(BF16),
            (targets & 255).astype(BF16),
            loss_weight,
        ],
        axis=1,
    )
    pay = jnp.concatenate([hidden, jnp.pad(digits, ((0, 0), (0, META - 4)))], axis=1)
    pay = from_everyone(pay, "z").reshape(NZ * OWN, -1)
    row = pay[:, : hidden.shape[1]]
    digits = pay[:, hidden.shape[1] :].astype(F32)
    target = digits[:, 0] * 65536.0 + digits[:, 1] * 256.0 + digits[:, 2]
    meta = from_everyone(jnp.stack([target, digits[:, 3]]), ("dp", "x", "core"))
    own = jnp.concatenate([row] + [shift(row, "x", -k) for k in range(1, NX)], axis=0)
    other = shift(own, "core", 1)
    return own, other, meta.reshape(NDP, NX, 2, 2, NZ * OWN)


def joined_stats(top, total):
    first = lax.axis_index("core") == 0
    place = lax.axis_index("x")

    def turned(stats, start):
        stats = jnp.where(first, stats, stats[:, ::-1])
        return lax.dynamic_slice_in_dim(jnp.concatenate([stats] * 2, axis=2), start, NX, 2)

    shape = (2, 2, NX, NZ * OWN)
    stats = turned(jnp.stack([top, total]).reshape(shape), lax.rem(NX - place, NX))
    every = from_everyone(stats.reshape(2, -1), ("x", "z", "core"))
    top = jnp.max(every[:, 0], axis=0)
    total = jnp.sum(every[:, 1] * jnp.exp(every[:, 0] - top), axis=0)
    stats = turned(jnp.stack([top, total]).reshape(shape), place).reshape(2, -1)
    return stats[0], stats[1]


def step(hidden, targets, loss_weight, head_weight, cluster_weight, tail_proj, tail_out):
    x_index, z_index, core_index = (lax.axis_index(a) for a in ("x", "z", "core"))
    vocab_index = lax.axis_index(("x", "z", "core"))
    dp_index = lax.axis_index("dp")
    model, width = head_weight.shape
    weight = jnp.concatenate([head_weight, cluster_weight], axis=1)
    own, other, meta = gathered(hidden, targets, loss_weight)
    side = own.shape[0]

    out = tail_out[0]
    part = out.shape[1] // NDP
    outs = []
    for k in range(NDP):
        piece = lax.dynamic_slice_in_dim(out, lax.rem(dp_index + k, NDP) * part, part, 1)
        outs.append(shift(piece, "dp", k) if k else piece)

    every_target = meta[:, :, :, 0].reshape(NDP, -1).astype(jnp.int32)
    every_gain = meta[:, :, :, 1].reshape(NDP, -1)
    offset = every_target - HEAD
    cluster = jnp.where(offset >= 0, offset // CV, -1)
    at = jnp.arange(cluster.shape[1], dtype=jnp.int32)
    earlier = (cluster[:, :, None] == cluster[:, None, :]) & (at[:, None] < at[None, :])
    rank = jnp.sum(earlier.astype(jnp.int32), axis=1)
    every_slot = jnp.where(cluster >= 0, cluster * CAP + rank, -1)
    caps = jnp.arange(CAP, dtype=jnp.int32)
    holds = every_slot[:, None, :] == vocab_index * CAP + caps[None, :, None]
    words = jnp.sum(jnp.where(holds, (offset % CV)[:, None, :], 0), axis=2).reshape(-1)
    gain_tail = jnp.sum(jnp.where(holds, every_gain[:, None, :], 0.0), axis=2).reshape(-1)

    block = jnp.stack([every_target.astype(F32), every_gain, every_slot.astype(F32)])
    block = lax.dynamic_index_in_dim(block, dp_index, 1, keepdims=False)
    block = block.reshape(3, NX, 2, NZ * OWN)
    block = lax.dynamic_slice_in_dim(jnp.concatenate([block] * 2, axis=1), x_index, NX, 1)
    block = jnp.where(core_index == 0, block, block[:, :, ::-1])
    block = jnp.swapaxes(block, 1, 2).reshape(3, -1)
    target = block[0].astype(jnp.int32)
    gain = block[1]
    slot = block[2].astype(jnp.int32)
    offset = target - HEAD

    select = (slot[None, :] == vocab_index * CAP + caps[:, None]).astype(BF16)
    picked = (dot(select[:, :side], own) + dot(select[:, side:], other)).astype(BF16)
    rows = from_everyone(picked, "dp").reshape(NDP * CAP, -1)
    proj = tail_proj[0]
    reduced = dot(rows, proj).astype(BF16)
    inner = [reduced] + [shift(reduced, "dp", k) for k in range(1, NDP)]
    share = dot(inner[0], outs[0])
    for k in range(1, NDP):
        share = share + dot(inner[k], outs[k])
    top = jnp.max(share, axis=1)
    total = jnp.sum(jnp.exp(share - top[:, None]), axis=1)
    every = from_everyone(jnp.stack([top, total]), "dp")
    top = jnp.max(every[:, 0], axis=0)
    total = jnp.sum(every[:, 1] * jnp.exp(every[:, 0] - top), axis=0)
    columns = dp_index * part + jnp.arange(part, dtype=jnp.int32)
    hot = (columns[None, :] == words[:, None]).astype(F32)
    share_delta = (
        gain_tail[:, None] * (jnp.exp(share - top[:, None]) / total[:, None] - hot)
    ).astype(BF16)
    reduced_grad = dot(share_delta, outs[0], 1, 1)
    for k in range(1, NDP):
        reduced_grad = reduced_grad + shift(dot(share_delta, outs[k], 1, 1), "dp", -k)
    reduced_grad = reduced_grad.astype(BF16)
    tail_partial = dot(reduced_grad, proj, 1, 1).astype(BF16)
    tail_sum = jnp.sum(
        swapped(tail_partial.reshape(NDP, CAP, model), "dp").astype(F32), axis=0
    ).astype(BF16)

    (own, other), _ = lax.optimization_barrier(((own, other), picked))
    logits = jnp.concatenate([dot(own, weight), dot(other, weight)], axis=0)
    lane = jnp.arange(width + 1, dtype=jnp.int32)
    columns = jnp.where(lane < width, vocab_index * width + lane, HEAD + vocab_index)
    target_column = jnp.where(offset >= 0, HEAD + offset // CV, target)
    top = jnp.max(logits, axis=1)
    total = jnp.sum(jnp.exp(logits - top[:, None]), axis=1)
    top, total = joined_stats(top, total)
    hot = (columns[None, :] == target_column[:, None]).astype(F32)
    delta = (
        gain[:, None] * (jnp.exp(logits - top[:, None]) / total[:, None] - hot)
    ).astype(BF16)
    near, far = delta[:side], delta[side:]
    far_part = dot(far, weight, 1, 1).astype(BF16)
    from_core = shift(far_part, "core", 1)
    pair = (dot(near, weight, 1, 1) + from_core.astype(F32)).reshape(NX, NZ * OWN, model)
    pair_16 = pair.astype(BF16)
    from_x = [shift(pair_16[k], "x", k) for k in range(1, NX)]
    chip = pair[0]
    for piece in from_x:
        chip = chip + piece.astype(F32)

    tail_all = [tail_sum] + [shift(tail_sum, "x", -k) for k in range(1, NX)]
    near_slot = slot.reshape(2, NX, NZ * OWN)[:, 0].reshape(-1)
    source_x = lax.rem(x_index + jnp.arange(NX, dtype=jnp.int32), NX)
    source = (source_x * NZ + z_index) * 2 + core_index
    source_slot = (source[:, None] * CAP + caps[None, :]).reshape(-1)
    place = (source_slot[:, None] == near_slot[None, :]).astype(BF16)
    tail_all = jnp.concatenate(tail_all, axis=0)
    rest = NZ * OWN
    far_tail = dot(place[:, rest:], tail_all, 0, 0).astype(BF16)
    tail_from_core = shift(far_tail, "core", 1)
    chip = chip + dot(place[:, :rest], tail_all, 0, 0) + tail_from_core.astype(F32)
    last = swapped(chip.reshape(NZ, OWN, model).astype(BF16), "z")
    hidden_grad = jnp.sum(last.astype(F32), axis=0).astype(BF16)

    grad_t = (dot(near, own, 0, 0) + dot(far, other, 0, 0)).astype(BF16)
    block = model // NDP
    pieces = [
        lax.dynamic_slice_in_dim(grad_t, lax.rem(dp_index + k, NDP) * block, block, 1)
        for k in range(NDP)
    ]
    arrived = [shift(pieces[k], "dp", k) for k in range(1, NDP)]
    head_sum = sum((p.astype(F32) for p in arrived), pieces[0].astype(F32)).astype(BF16)
    word_delta = from_everyone(share_delta, "dp")
    word_delta = jnp.swapaxes(word_delta, 0, 1).reshape(NDP * CAP, -1)
    out_grad = dot(reduced, word_delta, 0, 0).astype(BF16)
    proj_grad = dot(rows, reduced_grad, 0, 0).astype(BF16)
    return (
        hidden_grad,
        head_sum[:width].T,
        head_sum[width:].T,
        proj_grad[None],
        out_grad[None],
    )


def solution(mesh):
    fine = Mesh(mesh.devices.reshape(NDP, NX, NZ, 2), ("dp", "x", "z", "core"))
    vocab = ("x", "z", "core")
    return jax.shard_map(
        step,
        mesh=fine,
        in_specs=(
            P(("dp", *vocab), None),
            P(("dp", *vocab)),
            P(("dp", *vocab)),
            P(None, vocab),
            P(None, vocab),
            P(vocab, None, "dp"),
            P(vocab, "dp", None),
        ),
        out_specs=(
            P(("dp", *vocab), None),
            P("dp", vocab),
            P("dp", vocab),
            P(vocab, None, "dp"),
            P(vocab, "dp", None),
        ),
        check_vma=False,
    )
```

```python
import jax
import jax.numpy as jnp
from jax import lax
from jax.sharding import Mesh
from jax.sharding import PartitionSpec as P


HEAD = 10240
CV = 7680
CAP = 16
OWN = 8
NX, NZ, NDP = 4, 8, 4
META = 128
CA = 1408


F32, BF16 = jnp.float32, jnp.bfloat16


def shift(value, axis, step):
    n = lax.axis_size(axis)
    return lax.ppermute(value, axis, [(j, (j + step) % n) for j in range(n)])


def dot(a, b, ca=1, cb=0):
    return lax.dot_general(a, b, (((ca,), (cb,)), ((), ())), preferred_element_type=F32)


def swapped(parts, axis):
    return lax.all_to_all(parts, axis, split_axis=0, concat_axis=0, tiled=True)


def from_everyone(value, axis):
    return swapped(jnp.broadcast_to(value, (lax.axis_size(axis), *value.shape)), axis)


def gathered(hidden, targets, loss_weight):
    digits = jnp.stack(
        [
            (targets >> 16).astype(BF16),
            ((targets >> 8) & 255).astype(BF16),
            (targets & 255).astype(BF16),
            loss_weight,
        ],
        axis=1,
    )
    model = hidden.shape[1]
    rest = model - CA
    a1 = hidden[:, :CA]
    pay = jnp.concatenate([hidden[:, CA:], jnp.pad(digits, ((0, 0), (0, META - 4)))], axis=1)
    a1 = jnp.concatenate([a1] + [shift(a1, "x", -k) for k in range(1, NX)], axis=0)
    b1 = from_everyone(pay, "z").reshape(NZ * OWN, -1)
    a1, b1 = lax.optimization_barrier((a1, b1))
    a2 = from_everyone(a1, "z").reshape(NZ, NX, OWN, CA)
    b2 = [b1] + [shift(b1, "x", -k) for k in range(1, NX)]
    digits = jnp.stack([b[:, rest : rest + 4] for b in b2]).astype(F32)
    target = digits[..., 0] * 65536.0 + digits[..., 1] * 256.0 + digits[..., 2]
    meta = jnp.stack([target, digits[..., 3]])
    meta = jnp.stack([meta, shift(meta, "core", 1)], axis=1)
    own = jnp.zeros((NX * NZ * OWN, model), BF16)
    for k in range(NX):
        own = own.at[k * NZ * OWN : (k + 1) * NZ * OWN, CA:].set(b2[k][:, :rest])
    own = own.at[:, :CA].set(jnp.swapaxes(a2, 0, 1).reshape(-1, CA))
    other = shift(own, "core", 1)
    return own, other, meta.reshape(2, -1)


def joined_stats(top, total):
    first = lax.axis_index("core") == 0
    place = lax.axis_index("x")

    def turned(stats, start):
        stats = jnp.where(first, stats, stats[:, ::-1])
        return lax.dynamic_slice_in_dim(jnp.concatenate([stats] * 2, axis=2), start, NX, 2)

    shape = (2, 2, NX, NZ * OWN)
    stats = turned(jnp.stack([top, total]).reshape(shape), lax.rem(NX - place, NX))
    every = from_everyone(stats.reshape(2, -1), ("x", "z", "core"))
    top = jnp.max(every[:, 0], axis=0)
    total = jnp.sum(every[:, 1] * jnp.exp(every[:, 0] - top), axis=0)
    stats = turned(jnp.stack([top, total]).reshape(shape), place).reshape(2, -1)
    return stats[0], stats[1]


def step(hidden, targets, loss_weight, head_weight, cluster_weight, tail_proj, tail_out):
    x_index, z_index, core_index = (lax.axis_index(a) for a in ("x", "z", "core"))
    vocab_index = lax.axis_index(("x", "z", "core"))
    model, width = head_weight.shape
    weight = jnp.concatenate([head_weight, cluster_weight], axis=1)
    own, other, meta = gathered(hidden, targets, loss_weight)
    side = own.shape[0]

    target = meta[0].astype(jnp.int32)
    gain = meta[1]
    offset = target - HEAD
    cluster = jnp.where(offset >= 0, offset // CV, -1)
    core_at, x_at, z_at, row_at = jnp.unravel_index(jnp.arange(2 * side), (2, NX, NZ, OWN))
    x_at = lax.rem(x_at + x_index, NX)
    token = ((x_at * NZ + z_at) * 2 + lax.bitwise_xor(core_at, core_index)) * OWN + row_at
    earlier = (cluster[:, None] == cluster[None, :]) & (token[:, None] < token[None, :])
    rank = jnp.sum(earlier.astype(jnp.int32), axis=0)
    slot = jnp.where(cluster >= 0, cluster * CAP + rank, -1)
    caps = jnp.arange(CAP, dtype=jnp.int32)
    holds = slot[None, :] == vocab_index * CAP + caps[:, None]
    words = jnp.sum(jnp.where(holds, (offset % CV)[None, :], 0), axis=1)
    gain_tail = jnp.sum(jnp.where(holds, gain[None, :], 0.0), axis=1)

    select = holds.astype(BF16)
    picked = (dot(select[:, :side], own) + dot(select[:, side:], other)).astype(BF16)
    rows = from_everyone(picked, "dp")
    rows = lax.dynamic_slice_in_dim(jnp.concatenate([rows] * 2), lax.axis_index("dp"), NDP)
    rows = rows.reshape(NDP * CAP, -1)
    proj = tail_proj[0]
    out = tail_out[0]
    reduced = dot(rows, proj).astype(BF16)
    partial = dot(reduced, out)
    share = partial[:CAP]
    for k in range(1, NDP):
        share = share + shift(partial[k * CAP : (k + 1) * CAP], "dp", k)
    top = jnp.max(share, axis=1, keepdims=True)
    share_exp = jnp.exp(share - top)
    total = jnp.sum(share_exp, axis=1, keepdims=True)
    hot = (jnp.arange(CV, dtype=jnp.int32)[None, :] == words[:, None]).astype(F32)
    share_delta = (gain_tail[:, None] * (share_exp / total - hot)).astype(BF16)
    word_delta = jnp.concatenate(
        [share_delta] + [shift(share_delta, "dp", -k) for k in range(1, NDP)], axis=0
    )
    reduced_grad = dot(word_delta, out, 1, 1).astype(BF16)
    tail_partial = dot(reduced_grad, proj, 1, 1)
    tail_sum = tail_partial[:CAP]
    for k in range(1, NDP):
        piece = tail_partial[k * CAP : (k + 1) * CAP].astype(BF16)
        tail_sum = tail_sum + shift(piece, "dp", k).astype(F32)
    tail_sum = tail_sum.astype(BF16)

    (own, other), _ = lax.optimization_barrier(((own, other), picked))
    logits = jnp.concatenate([dot(own, weight), dot(other, weight)], axis=0)
    lane = jnp.arange(width + 1, dtype=jnp.int32)
    columns = jnp.where(lane < width, vocab_index * width + lane, HEAD + vocab_index)
    target_column = jnp.where(offset >= 0, HEAD + offset // CV, target)
    top = jnp.max(logits, axis=1)
    total = jnp.sum(jnp.exp(logits - top[:, None]), axis=1)
    top, total = joined_stats(top, total)
    hot = (columns[None, :] == target_column[:, None]).astype(F32)
    delta = (
        gain[:, None] * (jnp.exp(logits - top[:, None]) / total[:, None] - hot)
    ).astype(BF16)
    near, far = delta[:side], delta[side:]
    far_part = dot(far, weight, 1, 1).astype(BF16)
    from_core = shift(far_part, "core", 1)
    pair = (dot(near, weight, 1, 1) + from_core.astype(F32)).reshape(NX, NZ * OWN, model)
    pair_16 = pair.astype(BF16)
    from_x = [shift(pair_16[k], "x", k) for k in range(1, NX)]
    chip = pair[0]
    for piece in from_x:
        chip = chip + piece.astype(F32)

    tail_all = [tail_sum] + [shift(tail_sum, "x", -k) for k in range(1, NX)]
    near_slot = slot.reshape(2, NX, NZ * OWN)[:, 0].reshape(-1)
    source_x = lax.rem(x_index + jnp.arange(NX, dtype=jnp.int32), NX)
    source = (source_x * NZ + z_index) * 2 + core_index
    source_slot = (source[:, None] * CAP + caps[None, :]).reshape(-1)
    place = (source_slot[:, None] == near_slot[None, :]).astype(BF16)
    tail_all = jnp.concatenate(tail_all, axis=0)
    rest = NZ * OWN
    far_tail = dot(place[:, rest:], tail_all, 0, 0).astype(BF16)
    tail_from_core = shift(far_tail, "core", 1)
    chip = chip + dot(place[:, :rest], tail_all, 0, 0) + tail_from_core.astype(F32)
    last = swapped(chip.reshape(NZ, OWN, model).astype(BF16), "z")
    hidden_grad = jnp.sum(last.astype(F32), axis=0).astype(BF16)

    grad_t = (dot(near, own, 0, 0) + dot(far, other, 0, 0)).astype(BF16)
    grad_t = jnp.moveaxis(grad_t.reshape(width + 1, NDP, -1), 1, 0)
    grad_t = swapped(grad_t, "dp")
    head_sum = jnp.sum(grad_t.astype(F32), axis=0).astype(BF16)
    out_grad = dot(reduced, word_delta, 0, 0).astype(BF16)
    proj_grad = dot(rows, reduced_grad, 0, 0).astype(BF16)
    return (
        hidden_grad,
        head_sum[:width].T,
        head_sum[width:].T,
        proj_grad[None],
        out_grad[None],
    )


def solution(mesh):
    fine = Mesh(mesh.devices.reshape(NDP, NX, NZ, 2), ("dp", "x", "z", "core"))
    vocab = ("x", "z", "core")
    return jax.shard_map(
        step,
        mesh=fine,
        in_specs=(
            P(("dp", *vocab), None),
            P(("dp", *vocab)),
            P(("dp", *vocab)),
            P(None, vocab),
            P(None, vocab),
            P(vocab, None, "dp"),
            P(vocab, "dp", None),
        ),
        out_specs=(
            P(("dp", *vocab), None),
            P("dp", vocab),
            P("dp", vocab),
            P(vocab, None, "dp"),
            P(vocab, "dp", None),
        ),
        check_vma=False,
    )
```

```python
import jax
import jax.numpy as jnp
from jax import lax
from jax.sharding import Mesh
from jax.sharding import PartitionSpec as P


HEAD = 10240
CV = 7680
CAP = 16
OWN = 8
NX, NZ, NDP = 4, 8, 4
META = 128
CA = 1408


F32, BF16 = jnp.float32, jnp.bfloat16


def shift(value, axis, step):
    n = lax.axis_size(axis)
    return lax.ppermute(value, axis, [(j, (j + step) % n) for j in range(n)])


def dot(a, b, ca=1, cb=0):
    return lax.dot_general(a, b, (((ca,), (cb,)), ((), ())), preferred_element_type=F32)


def swapped(parts, axis):
    return lax.all_to_all(parts, axis, split_axis=0, concat_axis=0, tiled=True)


def from_everyone(value, axis):
    return swapped(jnp.broadcast_to(value, (lax.axis_size(axis), *value.shape)), axis)


def gathered(hidden, targets, loss_weight):
    digits = jnp.stack(
        [
            (targets >> 16).astype(BF16),
            ((targets >> 8) & 255).astype(BF16),
            (targets & 255).astype(BF16),
            loss_weight,
        ],
        axis=1,
    )
    model = hidden.shape[1]
    rest = model - CA
    a1 = hidden[:, :CA]
    pay = jnp.concatenate([hidden[:, CA:], jnp.pad(digits, ((0, 0), (0, META - 4)))], axis=1)
    a1 = jnp.concatenate([a1] + [shift(a1, "x", -k) for k in range(1, NX)], axis=0)
    b1 = from_everyone(pay, "z").reshape(NZ * OWN, -1)
    a1, b1 = lax.optimization_barrier((a1, b1))
    a2 = from_everyone(a1, "z").reshape(NZ, NX, OWN, CA)
    b2 = [b1] + [shift(b1, "x", -k) for k in range(1, NX)]
    digits = jnp.stack([b[:, rest : rest + 4] for b in b2]).astype(F32)
    target = digits[..., 0] * 65536.0 + digits[..., 1] * 256.0 + digits[..., 2]
    meta = jnp.stack([target, digits[..., 3]])
    meta = jnp.stack([meta, shift(meta, "core", 1)], axis=1)
    a2 = jnp.swapaxes(a2, 0, 1).reshape(-1, CA)
    own = jnp.concatenate([a2, jnp.concatenate(b2, axis=0)[:, :rest]], axis=1)
    other = shift(own, "core", 1)
    return own, other, meta.reshape(2, -1)


def joined_stats(top, total):
    first = lax.axis_index("core") == 0
    place = lax.axis_index("x")

    def turned(stats, start):
        stats = jnp.where(first, stats, stats[:, ::-1])
        return lax.dynamic_slice_in_dim(jnp.concatenate([stats] * 2, axis=2), start, NX, 2)

    shape = (2, 2, NX, NZ * OWN)
    stats = turned(jnp.stack([top, total]).reshape(shape), lax.rem(NX - place, NX))
    every = from_everyone(stats.reshape(2, -1), ("x", "z", "core"))
    top = jnp.max(every[:, 0], axis=0)
    total = jnp.sum(every[:, 1] * jnp.exp(every[:, 0] - top), axis=0)
    stats = turned(jnp.stack([top, total]).reshape(shape), place).reshape(2, -1)
    return stats[0], stats[1]


def step(hidden, targets, loss_weight, head_weight, cluster_weight, tail_proj, tail_out):
    x_index, z_index, core_index = (lax.axis_index(a) for a in ("x", "z", "core"))
    vocab_index = lax.axis_index(("x", "z", "core"))
    dp_index = lax.axis_index("dp")
    model, width = head_weight.shape
    weight = jnp.concatenate([head_weight, cluster_weight], axis=1)
    own, other, meta = gathered(hidden, targets, loss_weight)
    side = own.shape[0]

    target = meta[0].astype(jnp.int32)
    gain = meta[1]
    offset = target - HEAD
    cluster = jnp.where(offset >= 0, offset // CV, -1)
    core_at, x_at, z_at, row_at = jnp.unravel_index(jnp.arange(2 * side), (2, NX, NZ, OWN))
    x_at = lax.rem(x_at + x_index, NX)
    token = ((x_at * NZ + z_at) * 2 + lax.bitwise_xor(core_at, core_index)) * OWN + row_at
    earlier = (cluster[:, None] == cluster[None, :]) & (token[:, None] < token[None, :])
    rank = jnp.sum(earlier.astype(jnp.int32), axis=0)
    slot = jnp.where(cluster >= 0, cluster * CAP + rank, -1)
    caps = jnp.arange(CAP, dtype=jnp.int32)
    holds = slot[None, :] == vocab_index * CAP + caps[:, None]
    words = jnp.sum(jnp.where(holds, (offset % CV)[None, :], 0), axis=1)
    gain_tail = jnp.sum(jnp.where(holds, gain[None, :], 0.0), axis=1)

    select = holds.astype(BF16)
    picked = (dot(select[:, :side], own) + dot(select[:, side:], other)).astype(BF16)
    rows = from_everyone(picked, "dp")
    rows = rows.reshape(NDP * CAP, -1)
    proj = tail_proj[0]
    out = tail_out[0]
    reduced = dot(rows, proj).astype(BF16)
    partial = dot(reduced, out)

    def block(value, k, size, dim):
        return lax.dynamic_slice_in_dim(value, lax.rem(dp_index + k, NDP) * size, size, dim)

    share = block(partial, 0, CAP, 0)
    for k in range(1, NDP):
        share = share + shift(block(partial, k, CAP, 0), "dp", k)
    top = jnp.max(share, axis=1, keepdims=True)
    share_exp = jnp.exp(share - top)
    total = jnp.sum(share_exp, axis=1, keepdims=True)
    hot = (jnp.arange(CV, dtype=jnp.int32)[None, :] == words[:, None]).astype(F32)
    share_delta = (gain_tail[:, None] * (share_exp / total - hot)).astype(BF16)
    word_delta = from_everyone(share_delta, "dp").reshape(NDP * CAP, -1)
    reduced_grad = dot(word_delta, out, 1, 1).astype(BF16)
    tail_partial = dot(reduced_grad, proj, 1, 1)
    tail_sum = block(tail_partial, 0, CAP, 0)
    for k in range(1, NDP):
        piece = block(tail_partial, k, CAP, 0).astype(BF16)
        tail_sum = tail_sum + shift(piece, "dp", k).astype(F32)
    tail_sum = tail_sum.astype(BF16)

    (own, other), _ = lax.optimization_barrier(((own, other), picked))
    logits = jnp.concatenate([dot(own, weight), dot(other, weight)], axis=0)
    lane = jnp.arange(width + 1, dtype=jnp.int32)
    columns = jnp.where(lane < width, vocab_index * width + lane, HEAD + vocab_index)
    target_column = jnp.where(offset >= 0, HEAD + offset // CV, target)
    top = jnp.max(logits, axis=1)
    total = jnp.sum(jnp.exp(logits - top[:, None]), axis=1)
    top, total = joined_stats(top, total)
    hot = (columns[None, :] == target_column[:, None]).astype(F32)
    delta = (
        gain[:, None] * (jnp.exp(logits - top[:, None]) / total[:, None] - hot)
    ).astype(BF16)
    near, far = delta[:side], delta[side:]
    far_part = dot(far, weight, 1, 1).astype(BF16)
    from_core = shift(far_part, "core", 1)
    pair = (dot(near, weight, 1, 1) + from_core.astype(F32)).reshape(NX, NZ * OWN, model)
    pair_16 = pair.astype(BF16)
    from_x = [shift(pair_16[k], "x", k) for k in range(1, NX)]
    chip = pair[0]
    for piece in from_x:
        chip = chip + piece.astype(F32)

    tail_all = [tail_sum] + [shift(tail_sum, "x", -k) for k in range(1, NX)]
    near_slot = slot.reshape(2, NX, NZ * OWN)[:, 0].reshape(-1)
    source_x = lax.rem(x_index + jnp.arange(NX, dtype=jnp.int32), NX)
    source = (source_x * NZ + z_index) * 2 + core_index
    source_slot = (source[:, None] * CAP + caps[None, :]).reshape(-1)
    place = (source_slot[:, None] == near_slot[None, :]).astype(BF16)
    tail_all = jnp.concatenate(tail_all, axis=0)
    rest = NZ * OWN
    far_tail = dot(place[:, rest:], tail_all, 0, 0).astype(BF16)
    tail_from_core = shift(far_tail, "core", 1)
    chip = chip + dot(place[:, :rest], tail_all, 0, 0) + tail_from_core.astype(F32)
    last = swapped(chip.reshape(NZ, OWN, model).astype(BF16), "z")
    hidden_grad = jnp.sum(last.astype(F32), axis=0).astype(BF16)

    grad_t = (dot(near, own, 0, 0) + dot(far, other, 0, 0)).astype(BF16)
    pieces = [block(grad_t, k, model // NDP, 1) for k in range(NDP)]
    head_sum = pieces[0].astype(F32)
    for k in range(1, NDP):
        head_sum = head_sum + shift(pieces[k], "dp", k).astype(F32)
    head_sum = head_sum.astype(BF16)
    out_grad = dot(reduced, word_delta, 0, 0).astype(BF16)
    proj_grad = dot(rows, reduced_grad, 0, 0).astype(BF16)
    return (
        hidden_grad,
        head_sum[:width].T,
        head_sum[width:].T,
        proj_grad[None],
        out_grad[None],
    )


def solution(mesh):
    fine = Mesh(mesh.devices.reshape(NDP, NX, NZ, 2), ("dp", "x", "z", "core"))
    vocab = ("x", "z", "core")
    return jax.shard_map(
        step,
        mesh=fine,
        in_specs=(
            P(("dp", *vocab), None),
            P(("dp", *vocab)),
            P(("dp", *vocab)),
            P(None, vocab),
            P(None, vocab),
            P(vocab, None, "dp"),
            P(vocab, "dp", None),
        ),
        out_specs=(
            P(("dp", *vocab), None),
            P("dp", vocab),
            P("dp", vocab),
            P(vocab, None, "dp"),
            P(vocab, "dp", None),
        ),
        check_vma=False,
    )
```

```python
import jax
import jax.numpy as jnp
from jax import lax
from jax.sharding import Mesh
from jax.sharding import PartitionSpec as P


HEAD = 10240
CV = 7680
CAP = 16
OWN = 8
NX, NZ, NDP = 4, 8, 4
META = 128
CA = 1408


F32, BF16 = jnp.float32, jnp.bfloat16


def shift(value, axis, step):
    n = lax.axis_size(axis)
    return lax.ppermute(value, axis, [(j, (j + step) % n) for j in range(n)])


def dot(a, b, ca=1, cb=0):
    return lax.dot_general(a, b, (((ca,), (cb,)), ((), ())), preferred_element_type=F32)


def swapped(parts, axis):
    return lax.all_to_all(parts, axis, split_axis=0, concat_axis=0, tiled=True)


def from_everyone(value, axis):
    return swapped(jnp.broadcast_to(value, (lax.axis_size(axis), *value.shape)), axis)


def gathered(hidden, targets, loss_weight):
    digits = jnp.stack(
        [
            (targets >> 16).astype(BF16),
            ((targets >> 8) & 255).astype(BF16),
            (targets & 255).astype(BF16),
            loss_weight,
        ],
        axis=1,
    )
    model = hidden.shape[1]
    rest = model - CA
    a1 = hidden[:, :CA]
    pay = jnp.concatenate([hidden[:, CA:], jnp.pad(digits, ((0, 0), (0, META - 4)))], axis=1)
    a1 = jnp.concatenate([a1] + [shift(a1, "x", -k) for k in range(1, NX)], axis=0)
    b1 = from_everyone(pay, "z").reshape(NZ * OWN, -1)
    a1, b1 = lax.optimization_barrier((a1, b1))
    a2 = from_everyone(a1, "z").reshape(NZ, NX, OWN, CA)
    b2 = [b1] + [shift(b1, "x", -k) for k in range(1, NX)]
    own = jnp.zeros((NX * NZ * OWN, model + META), BF16)
    for k in range(NX):
        own = lax.dynamic_update_slice(own, b2[k], (k * NZ * OWN, 0))
    digits = own[:, rest : rest + META].astype(F32)
    target = digits[:, 0] * 65536.0 + digits[:, 1] * 256.0 + digits[:, 2]
    meta = jnp.stack([target, digits[:, 3]])
    meta = jnp.stack([meta, shift(meta, "core", 1)], axis=1)
    a2 = jnp.swapaxes(a2, 0, 1).reshape(-1, CA)
    own = lax.dynamic_update_slice(own, a2, (0, rest + META))
    other = shift(own, "core", 1)
    return own, other, meta.reshape(2, -1)


def mixed(weight):
    gap = jnp.zeros((META, weight.shape[1]), weight.dtype)
    return jnp.concatenate([weight[CA:], gap, weight[:CA]], axis=0)


def plain(value):
    split = value.shape[1] - CA
    return jnp.concatenate([value[:, split:], value[:, : split - META]], axis=1)


def joined_stats(top, total):
    first = lax.axis_index("core") == 0
    place = lax.axis_index("x")

    def turned(stats, start):
        stats = jnp.where(first, stats, stats[:, ::-1])
        return lax.dynamic_slice_in_dim(jnp.concatenate([stats] * 2, axis=2), start, NX, 2)

    shape = (2, 2, NX, NZ * OWN)
    stats = turned(jnp.stack([top, total]).reshape(shape), lax.rem(NX - place, NX))
    every = from_everyone(stats.reshape(2, -1), ("x", "z", "core"))
    top = jnp.max(every[:, 0], axis=0)
    total = jnp.sum(every[:, 1] * jnp.exp(every[:, 0] - top), axis=0)
    stats = turned(jnp.stack([top, total]).reshape(shape), place).reshape(2, -1)
    return stats[0], stats[1]


def step(hidden, targets, loss_weight, head_weight, cluster_weight, tail_proj, tail_out):
    x_index, z_index, core_index = (lax.axis_index(a) for a in ("x", "z", "core"))
    vocab_index = lax.axis_index(("x", "z", "core"))
    dp_index = lax.axis_index("dp")
    model, width = head_weight.shape
    weight = jnp.concatenate([head_weight, cluster_weight], axis=1)
    weight_mixed = mixed(weight)
    own, other, meta = gathered(hidden, targets, loss_weight)
    side = own.shape[0]

    target = meta[0].astype(jnp.int32)
    gain = meta[1]
    offset = target - HEAD
    cluster = jnp.where(offset >= 0, offset // CV, -1)
    core_at, x_at, z_at, row_at = jnp.unravel_index(jnp.arange(2 * side), (2, NX, NZ, OWN))
    x_at = lax.rem(x_at + x_index, NX)
    token = ((x_at * NZ + z_at) * 2 + lax.bitwise_xor(core_at, core_index)) * OWN + row_at
    earlier = (cluster[:, None] == cluster[None, :]) & (token[:, None] < token[None, :])
    rank = jnp.sum(earlier.astype(jnp.int32), axis=0)
    slot = jnp.where(cluster >= 0, cluster * CAP + rank, -1)
    caps = jnp.arange(CAP, dtype=jnp.int32)
    holds = slot[None, :] == vocab_index * CAP + caps[:, None]
    words = jnp.sum(jnp.where(holds, (offset % CV)[None, :], 0), axis=1)
    gain_tail = jnp.sum(jnp.where(holds, gain[None, :], 0.0), axis=1)

    select = holds.astype(BF16)
    picked = plain((dot(select[:, :side], own) + dot(select[:, side:], other)).astype(BF16))
    rows = from_everyone(picked, "dp")
    rows = rows.reshape(NDP * CAP, -1)
    proj = tail_proj[0]
    out = tail_out[0]
    reduced = dot(rows, proj).astype(BF16)
    partial = dot(reduced, out)

    def block(value, k, size, dim):
        return lax.dynamic_slice_in_dim(value, lax.rem(dp_index + k, NDP) * size, size, dim)

    share = block(partial, 0, CAP, 0)
    for k in range(1, NDP):
        share = share + shift(block(partial, k, CAP, 0), "dp", k)
    top = jnp.max(share, axis=1, keepdims=True)
    share_exp = jnp.exp(share - top)
    total = jnp.sum(share_exp, axis=1, keepdims=True)
    hot = (jnp.arange(CV, dtype=jnp.int32)[None, :] == words[:, None]).astype(F32)
    share_delta = (gain_tail[:, None] * (share_exp / total - hot)).astype(BF16)
    word_delta = jnp.concatenate(
        [share_delta] + [shift(share_delta, "dp", -k) for k in range(1, NDP)], axis=0
    )
    reduced_grad = dot(word_delta, out, 1, 1).astype(BF16)
    tail_partial = dot(reduced_grad, proj, 1, 1)
    tail_sum = tail_partial[:CAP]
    for k in range(1, NDP):
        piece = tail_partial[k * CAP : (k + 1) * CAP].astype(BF16)
        tail_sum = tail_sum + shift(piece, "dp", k).astype(F32)
    tail_sum = tail_sum.astype(BF16)

    (own, other), _ = lax.optimization_barrier(((own, other), picked))
    logits = jnp.concatenate([dot(own, weight_mixed), dot(other, weight_mixed)], axis=0)
    lane = jnp.arange(width + 1, dtype=jnp.int32)
    columns = jnp.where(lane < width, vocab_index * width + lane, HEAD + vocab_index)
    target_column = jnp.where(offset >= 0, HEAD + offset // CV, target)
    top = jnp.max(logits, axis=1)
    total = jnp.sum(jnp.exp(logits - top[:, None]), axis=1)
    top, total = joined_stats(top, total)
    hot = (columns[None, :] == target_column[:, None]).astype(F32)
    delta = (
        gain[:, None] * (jnp.exp(logits - top[:, None]) / total[:, None] - hot)
    ).astype(BF16)
    near, far = delta[:side], delta[side:]
    far_part = dot(far, weight, 1, 1).astype(BF16)
    from_core = shift(far_part, "core", 1)
    pair = (dot(near, weight, 1, 1) + from_core.astype(F32)).reshape(NX, NZ * OWN, model)
    pair_16 = pair.astype(BF16)
    from_x = [shift(pair_16[k], "x", k) for k in range(1, NX)]
    chip = pair[0]
    for piece in from_x:
        chip = chip + piece.astype(F32)

    tail_all = [tail_sum] + [shift(tail_sum, "x", -k) for k in range(1, NX)]
    near_slot = slot.reshape(2, NX, NZ * OWN)[:, 0].reshape(-1)
    source_x = lax.rem(x_index + jnp.arange(NX, dtype=jnp.int32), NX)
    source = (source_x * NZ + z_index) * 2 + core_index
    source_slot = (source[:, None] * CAP + caps[None, :]).reshape(-1)
    place = (source_slot[:, None] == near_slot[None, :]).astype(BF16)
    tail_all = jnp.concatenate(tail_all, axis=0)
    rest = NZ * OWN
    far_tail = dot(place[:, rest:], tail_all, 0, 0).astype(BF16)
    tail_from_core = shift(far_tail, "core", 1)
    chip = chip + dot(place[:, :rest], tail_all, 0, 0) + tail_from_core.astype(F32)
    last = swapped(chip.reshape(NZ, OWN, model).astype(BF16), "z")
    hidden_grad = jnp.sum(last.astype(F32), axis=0).astype(BF16)

    grad_t = (dot(near, own, 0, 0) + dot(far, other, 0, 0)).astype(BF16)
    grad_t = plain(grad_t)
    pieces = [block(grad_t, k, model // NDP, 1) for k in range(NDP)]
    head_sum = pieces[0].astype(F32)
    for k in range(1, NDP):
        head_sum = head_sum + shift(pieces[k], "dp", k).astype(F32)
    head_sum = head_sum.astype(BF16)

    def turned(value):
        return lax.dynamic_slice_in_dim(
            jnp.concatenate([value] * 2), dp_index * CAP, NDP * CAP
        )

    out_grad = dot(turned(reduced), word_delta, 0, 0).astype(BF16)
    proj_grad = dot(turned(rows), reduced_grad, 0, 0).astype(BF16)
    return (
        hidden_grad,
        head_sum[:width].T,
        head_sum[width:].T,
        proj_grad[None],
        out_grad[None],
    )


def solution(mesh):
    fine = Mesh(mesh.devices.reshape(NDP, NX, NZ, 2), ("dp", "x", "z", "core"))
    vocab = ("x", "z", "core")
    return jax.shard_map(
        step,
        mesh=fine,
        in_specs=(
            P(("dp", *vocab), None),
            P(("dp", *vocab)),
            P(("dp", *vocab)),
            P(None, vocab),
            P(None, vocab),
            P(vocab, None, "dp"),
            P(vocab, "dp", None),
        ),
        out_specs=(
            P(("dp", *vocab), None),
            P("dp", vocab),
            P("dp", vocab),
            P(vocab, None, "dp"),
            P(vocab, "dp", None),
        ),
        check_vma=False,
    )
```

```python
import jax
import jax.numpy as jnp
from jax import lax
from jax.sharding import Mesh
from jax.sharding import PartitionSpec as P


HEAD = 10240
CV = 7680
CAP = 16
OWN = 8
NX, NZ, NDP = 4, 8, 4
META = 128
CA = 1536


F32, BF16 = jnp.float32, jnp.bfloat16


def shift(value, axis, step):
    n = lax.axis_size(axis)
    return lax.ppermute(value, axis, [(j, (j + step) % n) for j in range(n)])


def swap(value, axis, bits):
    n = lax.axis_size(axis)
    return lax.ppermute(value, axis, [(j, j ^ bits) for j in range(n)])


def dot(a, b, ca=1, cb=0):
    return lax.dot_general(a, b, (((ca,), (cb,)), ((), ())), preferred_element_type=F32)


def swapped(parts, axis):
    return lax.all_to_all(parts, axis, split_axis=0, concat_axis=0, tiled=True)


def from_everyone(value, axis):
    return swapped(jnp.broadcast_to(value, (lax.axis_size(axis), *value.shape)), axis)


def gathered(hidden, targets, loss_weight):
    digits = jnp.stack(
        [
            (targets >> 16).astype(BF16),
            ((targets >> 8) & 255).astype(BF16),
            (targets & 255).astype(BF16),
            loss_weight,
        ],
        axis=1,
    )
    model = hidden.shape[1]
    rest = model - CA
    a1 = hidden[:, :CA]
    pay = jnp.concatenate([hidden[:, CA:], jnp.pad(digits, ((0, 0), (0, META - 4)))], axis=1)
    a1 = jnp.concatenate([a1, swap(a1, "x", 1)], axis=0)
    a1 = jnp.concatenate([a1, swap(a1, "x", 2)], axis=0)
    b1 = from_everyone(pay, "z").reshape(NZ * OWN, -1)
    a1, b1 = lax.optimization_barrier((a1, b1))
    a2 = from_everyone(a1, "z").reshape(NZ, NX, OWN, CA)
    b2 = [b1] + [swap(b1, "x", k) for k in range(1, NX)]
    own = jnp.zeros((NX * NZ * OWN, model + META), BF16)
    for k in range(NX):
        own = lax.dynamic_update_slice(own, b2[k], (k * NZ * OWN, 0))
    digits = own[:, rest : rest + META].astype(F32)
    target = digits[:, 0] * 65536.0 + digits[:, 1] * 256.0 + digits[:, 2]
    meta = jnp.stack([target, digits[:, 3]])
    meta = jnp.stack([meta, shift(meta, "core", 1)], axis=1)
    a2 = jnp.swapaxes(a2, 0, 1).reshape(-1, CA)
    own = lax.dynamic_update_slice(own, a2, (0, rest + META))
    other = shift(own, "core", 1)
    return own, other, meta.reshape(2, -1)


def mixed(weight):
    gap = jnp.zeros((META, weight.shape[1]), weight.dtype)
    return jnp.concatenate([weight[CA:], gap, weight[:CA]], axis=0)


def plain(value):
    split = value.shape[1] - CA
    return jnp.concatenate([value[:, split:], value[:, : split - META]], axis=1)


def joined_stats(top, total):
    core, place = lax.axis_index("core"), lax.axis_index("x")

    def turned(stats):
        stats = stats.reshape(2, 2, 2, 2, NZ * OWN)
        stats = jnp.where(core == 0, stats, stats[:, ::-1])
        stats = jnp.where(place < 2, stats, stats[:, :, ::-1])
        return jnp.where(place % 2 == 0, stats, stats[:, :, :, ::-1])

    stats = turned(jnp.stack([top, total]))
    every = from_everyone(stats.reshape(2, -1), ("x", "z", "core"))
    top = jnp.max(every[:, 0], axis=0)
    total = jnp.sum(every[:, 1] * jnp.exp(every[:, 0] - top), axis=0)
    stats = turned(jnp.stack([top, total])).reshape(2, -1)
    return stats[0], stats[1]


def step(hidden, targets, loss_weight, head_weight, cluster_weight, tail_proj, tail_out):
    x_index, z_index, core_index = (lax.axis_index(a) for a in ("x", "z", "core"))
    vocab_index = lax.axis_index(("x", "z", "core"))
    dp_index = lax.axis_index("dp")
    model, width = head_weight.shape
    weight = jnp.concatenate([head_weight, cluster_weight], axis=1)
    weight_mixed = mixed(weight)
    own, other, meta = gathered(hidden, targets, loss_weight)
    side = own.shape[0]

    target = meta[0].astype(jnp.int32)
    gain = meta[1]
    offset = target - HEAD
    cluster = jnp.where(offset >= 0, offset // CV, -1)
    core_at, x_at, z_at, row_at = jnp.unravel_index(jnp.arange(2 * side), (2, NX, NZ, OWN))
    x_at = lax.bitwise_xor(x_at, x_index)
    token = ((x_at * NZ + z_at) * 2 + lax.bitwise_xor(core_at, core_index)) * OWN + row_at
    earlier = (cluster[:, None] == cluster[None, :]) & (token[:, None] < token[None, :])
    rank = jnp.sum(earlier.astype(jnp.int32), axis=0)
    slot = jnp.where(cluster >= 0, cluster * CAP + rank, -1)
    caps = jnp.arange(CAP, dtype=jnp.int32)
    holds = slot[None, :] == vocab_index * CAP + caps[:, None]
    words = jnp.sum(jnp.where(holds, (offset % CV)[None, :], 0), axis=1)
    gain_tail = jnp.sum(jnp.where(holds, gain[None, :], 0.0), axis=1)

    select = holds.astype(BF16)
    picked = plain((dot(select[:, :side], own) + dot(select[:, side:], other)).astype(BF16))
    rows = jnp.concatenate([picked] + [shift(picked, "dp", -k) for k in range(1, NDP)], axis=0)
    proj = tail_proj[0]
    out = tail_out[0]
    reduced = dot(rows, proj).astype(BF16)
    partial = dot(reduced, out)

    share = partial[:CAP]
    for k in range(1, NDP):
        share = share + shift(partial[k * CAP : (k + 1) * CAP], "dp", k)
    top = jnp.max(share, axis=1, keepdims=True)
    share_exp = jnp.exp(share - top)
    total = jnp.sum(share_exp, axis=1, keepdims=True)
    hot = (jnp.arange(CV, dtype=jnp.int32)[None, :] == words[:, None]).astype(F32)
    share_delta = (gain_tail[:, None] * (share_exp / total - hot)).astype(BF16)
    word_delta = jnp.concatenate(
        [share_delta] + [shift(share_delta, "dp", -k) for k in range(1, NDP)], axis=0
    )
    reduced_grad = dot(word_delta, out, 1, 1).astype(BF16)
    tail_partial = dot(reduced_grad, proj, 1, 1)
    tail_sum = tail_partial[:CAP]
    for k in range(1, NDP):
        piece = tail_partial[k * CAP : (k + 1) * CAP].astype(BF16)
        tail_sum = tail_sum + shift(piece, "dp", k).astype(F32)
    tail_sum = tail_sum.astype(BF16)

    (own, other), _ = lax.optimization_barrier(((own, other), picked))
    logits = jnp.concatenate([dot(own, weight_mixed), dot(other, weight_mixed)], axis=0)
    lane = jnp.arange(width + 1, dtype=jnp.int32)
    columns = jnp.where(lane < width, vocab_index * width + lane, HEAD + vocab_index)
    target_column = jnp.where(offset >= 0, HEAD + offset // CV, target)
    top = jnp.max(logits, axis=1)
    total = jnp.sum(jnp.exp(logits - top[:, None]), axis=1)
    top, total = joined_stats(top, total)
    hot = (columns[None, :] == target_column[:, None]).astype(F32)
    delta = (
        gain[:, None] * (jnp.exp(logits - top[:, None]) / total[:, None] - hot)
    ).astype(BF16)
    near, far = delta[:side], delta[side:]
    far_part = dot(far, weight, 1, 1).astype(BF16)
    from_core = shift(far_part, "core", 1)
    pair = (dot(near, weight, 1, 1) + from_core.astype(F32)).reshape(NX, NZ * OWN, model)
    pair_16 = pair.astype(BF16)
    from_x = [swap(pair_16[k], "x", k) for k in range(1, NX)]
    chip = pair[0]
    for piece in from_x:
        chip = chip + piece.astype(F32)

    tail_all = [tail_sum] + [swap(tail_sum, "x", k) for k in range(1, NX)]
    near_slot = slot.reshape(2, NX, NZ * OWN)[:, 0].reshape(-1)
    source_x = lax.bitwise_xor(x_index, jnp.arange(NX, dtype=jnp.int32))
    source = (source_x * NZ + z_index) * 2 + core_index
    source_slot = (source[:, None] * CAP + caps[None, :]).reshape(-1)
    place = (source_slot[:, None] == near_slot[None, :]).astype(BF16)
    tail_all = jnp.concatenate(tail_all, axis=0)
    rest = NZ * OWN
    far_tail = dot(place[:, rest:], tail_all, 0, 0).astype(BF16)
    tail_from_core = shift(far_tail, "core", 1)
    chip = lax.optimization_barrier(chip + dot(place[:, :rest], tail_all, 0, 0))
    chip = chip + tail_from_core.astype(F32)
    last = swapped(chip.reshape(NZ, OWN, model).astype(BF16), "z")
    hidden_grad = jnp.sum(last.astype(F32), axis=0).astype(BF16)

    grad_t = (dot(near, own, 0, 0) + dot(far, other, 0, 0)).astype(BF16)
    grad_t = plain(grad_t)
    block = model // NDP
    pieces = [
        lax.dynamic_slice_in_dim(grad_t, lax.bitwise_xor(dp_index, k) * block, block, 1)
        for k in range(NDP)
    ]
    pair = jnp.stack([pieces[1], pieces[3]])
    pair = swap(pair, "dp", 1).astype(F32)
    near_sum = pieces[0].astype(F32) + pair[0]
    far_sum = (pieces[2].astype(F32) + pair[1]).astype(BF16)
    far_sum = swap(far_sum, "dp", 2).astype(F32)
    head_sum = (near_sum + far_sum).astype(BF16)
    out_grad = dot(reduced, word_delta, 0, 0).astype(BF16)
    proj_grad = dot(rows, reduced_grad, 0, 0).astype(BF16)
    return (
        hidden_grad,
        head_sum[:width].T,
        head_sum[width:].T,
        proj_grad[None],
        out_grad[None],
    )


def solution(mesh):
    fine = Mesh(mesh.devices.reshape(NDP, NX, NZ, 2), ("dp", "x", "z", "core"))
    vocab = ("x", "z", "core")
    return jax.shard_map(
        step,
        mesh=fine,
        in_specs=(
            P(("dp", *vocab), None),
            P(("dp", *vocab)),
            P(("dp", *vocab)),
            P(None, vocab),
            P(None, vocab),
            P(vocab, None, "dp"),
            P(vocab, "dp", None),
        ),
        out_specs=(
            P(("dp", *vocab), None),
            P("dp", vocab),
            P("dp", vocab),
            P(vocab, None, "dp"),
            P(vocab, "dp", None),
        ),
        check_vma=False,
    )
```

```python
import jax
import jax.numpy as jnp
from jax import lax
from jax.sharding import Mesh
from jax.sharding import PartitionSpec as P


HEAD = 10240
CV = 7680
CAP = 16
OWN = 8
NX, NZ, NDP = 4, 8, 4
META = 128
CA = 1536


F32, BF16 = jnp.float32, jnp.bfloat16


def shift(value, axis, step):
    n = lax.axis_size(axis)
    return lax.ppermute(value, axis, [(j, (j + step) % n) for j in range(n)])


def dot(a, b, ca=1, cb=0):
    return lax.dot_general(a, b, (((ca,), (cb,)), ((), ())), preferred_element_type=F32)


def swapped(parts, axis):
    return lax.all_to_all(parts, axis, split_axis=0, concat_axis=0, tiled=True)


def from_everyone(value, axis):
    return swapped(jnp.broadcast_to(value, (lax.axis_size(axis), *value.shape)), axis)


def gathered(hidden, targets, loss_weight):
    lane = jnp.arange(META, dtype=jnp.int32)
    digit = (targets[:, None] >> jnp.maximum(16 - 8 * lane, 0)[None, :]) & 255
    digits = jnp.where(lane[None, :] == 3, loss_weight[:, None], digit.astype(BF16))
    model = hidden.shape[1]
    rest = model - CA
    a1 = hidden[:, :CA]
    pay = jnp.concatenate([hidden[:, CA:], digits], axis=1)
    a1 = jnp.concatenate([a1] + [shift(a1, "x", -k) for k in range(1, NX)], axis=0)
    b1 = from_everyone(pay, "z").reshape(NZ * OWN, -1)
    a1, b1 = lax.optimization_barrier((a1, b1))
    a2 = from_everyone(a1, "z").reshape(NZ, NX, OWN, CA)
    b2 = [b1] + [shift(b1, "x", -k) for k in range(1, NX)]
    own = jnp.zeros((NX * NZ * OWN, model + META), BF16)
    for k in range(NX):
        own = lax.dynamic_update_slice(own, b2[k], (k * NZ * OWN, 0))
    digits = own[:, rest : rest + META].astype(F32)
    target = digits[:, 0] * 65536.0 + digits[:, 1] * 256.0 + digits[:, 2]
    meta = jnp.stack([target, digits[:, 3]])
    meta = jnp.stack([meta, shift(meta, "core", 1)], axis=1)
    a2 = jnp.swapaxes(a2, 0, 1).reshape(-1, CA)
    own = lax.dynamic_update_slice(own, a2, (0, rest + META))
    other = shift(own, "core", 1)
    return own, other, meta.reshape(2, -1)


def mixed(weight):
    gap = jnp.zeros((META, weight.shape[1]), weight.dtype)
    return jnp.concatenate([weight[CA:], gap, weight[:CA]], axis=0)


def plain(value):
    split = value.shape[1] - CA
    return jnp.concatenate([value[:, split:], value[:, : split - META]], axis=1)


def joined_stats(top, total):
    first = lax.axis_index("core") == 0
    place = lax.axis_index("x")

    def turned(stats, start):
        stats = jnp.where(first, stats, stats[:, ::-1])
        return lax.dynamic_slice_in_dim(jnp.concatenate([stats] * 2, axis=2), start, NX, 2)

    shape = (2, 2, NX, NZ * OWN)
    stats = turned(jnp.stack([top, total]).reshape(shape), lax.rem(NX - place, NX))
    every = from_everyone(stats.reshape(2, -1), ("x", "z", "core"))
    top = jnp.max(every[:, 0], axis=0)
    total = jnp.sum(every[:, 1] * jnp.exp(every[:, 0] - top), axis=0)
    stats = turned(jnp.stack([top, total]).reshape(shape), place).reshape(2, -1)
    return stats[0], stats[1]


def step(hidden, targets, loss_weight, head_weight, cluster_weight, tail_proj, tail_out):
    x_index, z_index, core_index = (lax.axis_index(a) for a in ("x", "z", "core"))
    vocab_index = lax.axis_index(("x", "z", "core"))
    dp_index = lax.axis_index("dp")
    model, width = head_weight.shape
    weight = jnp.concatenate([head_weight, cluster_weight], axis=1)
    weight_mixed = mixed(weight)
    own, other, meta = gathered(hidden, targets, loss_weight)
    side = own.shape[0]

    target = meta[0].astype(jnp.int32)
    gain = meta[1]
    offset = target - HEAD
    cluster = jnp.where(offset >= 0, offset // CV, -1)
    core_at, x_at, z_at, row_at = jnp.unravel_index(jnp.arange(2 * side), (2, NX, NZ, OWN))
    x_at = lax.rem(x_at + x_index, NX)
    token = ((x_at * NZ + z_at) * 2 + lax.bitwise_xor(core_at, core_index)) * OWN + row_at
    earlier = (cluster[:, None] == cluster[None, :]) & (token[:, None] < token[None, :])
    rank = jnp.sum(earlier.astype(jnp.int32), axis=0)
    slot = jnp.where(cluster >= 0, cluster * CAP + rank, -1)
    caps = jnp.arange(CAP, dtype=jnp.int32)
    holds = slot[None, :] == vocab_index * CAP + caps[:, None]
    words = jnp.sum(jnp.where(holds, (offset % CV)[None, :], 0), axis=1)
    gain_tail = jnp.sum(jnp.where(holds, gain[None, :], 0.0), axis=1)

    select = holds.astype(BF16)
    picked = plain((dot(select[:, :side], own) + dot(select[:, side:], other)).astype(BF16))
    rows = from_everyone(picked, "dp")
    rows = rows.reshape(NDP * CAP, -1)
    proj = tail_proj[0]
    out = tail_out[0]
    reduced = dot(rows, proj).astype(BF16)
    partial = dot(reduced, out)

    def block(value, k, size, dim):
        return lax.dynamic_slice_in_dim(value, lax.rem(dp_index + k, NDP) * size, size, dim)

    share = block(partial, 0, CAP, 0)
    for k in range(1, NDP):
        share = share + shift(block(partial, k, CAP, 0), "dp", k)
    top = jnp.max(share, axis=1, keepdims=True)
    share_exp = jnp.exp(share - top)
    total = jnp.sum(share_exp, axis=1, keepdims=True)
    hot = (jnp.arange(CV, dtype=jnp.int32)[None, :] == words[:, None]).astype(F32)
    share_delta = (gain_tail[:, None] * (share_exp / total - hot)).astype(BF16)
    word_delta = jnp.concatenate(
        [share_delta] + [shift(share_delta, "dp", -k) for k in range(1, NDP)], axis=0
    )
    reduced_grad = dot(word_delta, out, 1, 1).astype(BF16)
    tail_partial = dot(reduced_grad, proj, 1, 1)
    tail_sum = tail_partial[:CAP]
    for k in range(1, NDP):
        piece = tail_partial[k * CAP : (k + 1) * CAP].astype(BF16)
        tail_sum = tail_sum + shift(piece, "dp", k).astype(F32)
    tail_sum = tail_sum.astype(BF16)

    (own, other), _ = lax.optimization_barrier(((own, other), picked))
    logits = jnp.concatenate([dot(own, weight_mixed), dot(other, weight_mixed)], axis=0)
    lane = jnp.arange(width + 1, dtype=jnp.int32)
    columns = jnp.where(lane < width, vocab_index * width + lane, HEAD + vocab_index)
    target_column = jnp.where(offset >= 0, HEAD + offset // CV, target)
    top = jnp.max(logits, axis=1)
    total = jnp.sum(jnp.exp(logits - top[:, None]), axis=1)
    top, total = joined_stats(top, total)
    hot = (columns[None, :] == target_column[:, None]).astype(F32)
    delta = (
        gain[:, None] * (jnp.exp(logits - top[:, None]) / total[:, None] - hot)
    ).astype(BF16)
    near, far = delta[:side], delta[side:]
    far_part = dot(far, weight, 1, 1).astype(BF16)
    from_core = shift(far_part, "core", 1)
    pair = (dot(near, weight, 1, 1) + from_core.astype(F32)).reshape(NX, NZ * OWN, model)
    pair_16 = pair.astype(BF16)
    from_x = [shift(pair_16[k], "x", k) for k in range(1, NX)]
    chip = pair[0]
    for piece in from_x:
        chip = chip + piece.astype(F32)

    tail_all = [tail_sum] + [shift(tail_sum, "x", -k) for k in range(1, NX)]
    near_slot = slot.reshape(2, NX, NZ * OWN)[:, 0].reshape(-1)
    source_x = lax.rem(x_index + jnp.arange(NX, dtype=jnp.int32), NX)
    source = (source_x * NZ + z_index) * 2 + core_index
    source_slot = (source[:, None] * CAP + caps[None, :]).reshape(-1)
    place = (source_slot[:, None] == near_slot[None, :]).astype(BF16)
    tail_all = jnp.concatenate(tail_all, axis=0)
    rest = NZ * OWN
    far_tail = dot(place[:, rest:], tail_all, 0, 0).astype(BF16)
    tail_from_core = shift(far_tail, "core", 1)
    chip = lax.optimization_barrier(chip + dot(place[:, :rest], tail_all, 0, 0))
    chip = chip + tail_from_core.astype(F32)
    last = swapped(chip.reshape(NZ, OWN, model).astype(BF16), "z")
    hidden_grad = jnp.sum(last.astype(F32), axis=0).astype(BF16)

    grad_t = (dot(near, own, 0, 0) + dot(far, other, 0, 0)).astype(BF16)
    grad_t = plain(grad_t)
    pieces = [block(grad_t, k, model // NDP, 1) for k in range(NDP)]
    head_sum = pieces[0].astype(F32)
    for k in range(1, NDP):
        head_sum = head_sum + shift(pieces[k], "dp", k).astype(F32)
    head_sum = head_sum.astype(BF16)

    def turned(value):
        return lax.dynamic_slice_in_dim(
            jnp.concatenate([value] * 2), dp_index * CAP, NDP * CAP
        )

    out_grad = dot(turned(reduced), word_delta, 0, 0).astype(BF16)
    proj_grad = dot(turned(rows), reduced_grad, 0, 0).astype(BF16)
    return (
        hidden_grad,
        head_sum[:width].T,
        head_sum[width:].T,
        proj_grad[None],
        out_grad[None],
    )


def solution(mesh):
    fine = Mesh(mesh.devices.reshape(NDP, NX, NZ, 2), ("dp", "x", "z", "core"))
    vocab = ("x", "z", "core")
    return jax.shard_map(
        step,
        mesh=fine,
        in_specs=(
            P(("dp", *vocab), None),
            P(("dp", *vocab)),
            P(("dp", *vocab)),
            P(None, vocab),
            P(None, vocab),
            P(vocab, None, "dp"),
            P(vocab, "dp", None),
        ),
        out_specs=(
            P(("dp", *vocab), None),
            P("dp", vocab),
            P("dp", vocab),
            P(vocab, None, "dp"),
            P(vocab, "dp", None),
        ),
        check_vma=False,
    )
```
